512 devices in a mesh: row: 16 (over z_hi, x), col: 32 (over y, z_lo, core).
Axes of the slice: x: 4, y: 4, z: 16 (z_hi: 4, z_lo: 4; z = z_hi * 4 + z_lo), core: 2. Of those that a mesh axis runs over, the one named last changes fastest.
Arguments:
- points: bfloat16 [32768, 768], P(('row', 'col')), may hold values from -8 to 8
- assign: int32 [32768], P(('row', 'col')), may hold values from 0 to 4095, as said below
Outputs:
- distance: float32 [32768, 4096], P('row', 'col')
The draws below stay inside these ranges and needn't reach their ends.
Inputs may be any that keep to these rules, and one draw needn't show every extreme that they name: Cluster group of a point is assign // 128. Among the 64 points of one device (aligned blocks of 64) at most 4 fall in one cluster group, and in every such block some group has exactly 4.
All inputs are finite; a program needn't handle non-finite values.
Results may differ from the reference program's by a relative error of at most 0.0003.
Values may be sent and summed in bfloat16 or wider, within the bound.
A program may use at most 64 MiB of HBM per device.

```python
import jax
import jax.numpy as jnp
from jax import lax

D = 768
CL_DEV = 128
P_DEV = 64
SLOT = 4
CL = 4096
NPTS = 32768


def make_assign(key):
    key = jax.random.fold_in(key, 17)
    blocks = NPTS // P_DEV
    group_count = CL // CL_DEV
    pool_size = group_count * SLOT
    key_favor, key_score, key_forced, key_shuffle, key_local = jax.random.split(key, 5)
    favored = jax.random.randint(key_favor, (group_count,), 0, 2 ** 16)
    pool_group = jnp.arange(pool_size, dtype=jnp.int32) // SLOT
    scores = jax.random.randint(key_score, (blocks, pool_size), 0, 2 ** 16) + favored[pool_group][None, :]
    scores = scores * pool_size + jnp.arange(pool_size, dtype=jnp.int32)[None, :]
    forced = jax.random.randint(key_forced, (blocks,), 0, group_count)
    scores = jnp.where(pool_group[None, :] == forced[:, None], jnp.arange(pool_size, dtype=jnp.int32)[None, :] - 2 * pool_size, scores)
    chosen = jnp.argsort(scores, axis=1, stable=True)[:, :P_DEV]
    groups_drawn = chosen // SLOT
    shuffle_keys = jax.random.randint(key_shuffle, (blocks, P_DEV), 0, 2 ** 16) * P_DEV + jnp.arange(P_DEV, dtype=jnp.int32)[None, :]
    shuffle = jnp.argsort(shuffle_keys, axis=1, stable=True)
    groups_drawn = jnp.take_along_axis(groups_drawn, shuffle, axis=1)
    local_ids = jax.random.randint(key_local, (blocks, P_DEV), 0, CL_DEV)
    return (groups_drawn * CL_DEV + local_ids).reshape(NPTS).astype(jnp.int32)


def draw_assign(key, part=0):
    return make_assign(key)


def draw_points(key, part=0):
    assign = make_assign(key)
    key_centre = jax.random.fold_in(jax.random.fold_in(key, 29), 0)
    key_basis = jax.random.fold_in(jax.random.fold_in(key, 29), 2)
    key_latent = jax.random.fold_in(jax.random.fold_in(key, 29), 3)
    key_noise = jax.random.fold_in(jax.random.fold_in(key, 29), 4)
    latent_dims = 4
    latent_scale = 0.5
    noise_scale = 0.5
    basis = jax.random.normal(key_basis, (latent_dims, D), jnp.float32)
    centres = jax.random.normal(key_centre, (CL, D), jnp.float32)
    latent = jax.random.normal(key_latent, (NPTS, latent_dims), jnp.float32) * latent_scale
    noise = jax.random.normal(key_noise, (NPTS, D), jnp.float32) * noise_scale
    values = centres[assign] + jnp.dot(latent, basis) + noise
    return jnp.clip(values, -8.0, 8.0).astype(jnp.bfloat16)


def setup_inputs(seed: int = 0) -> dict:
    key_of = jax.random.split(jax.random.key(seed), 3)
    return {
        "points": draw_points(jax.random.fold_in(key_of[2], 71), 0),
        "assign": draw_assign(jax.random.fold_in(key_of[2], 71), 0),
    }


def squares(values):
    return jnp.sum(jnp.square(values.astype(jnp.float32)), axis=1)


def reference(points, assign):
    indicator = (assign[:, None] == jnp.arange(CL, dtype=jnp.int32)[None, :]).astype(jnp.bfloat16)
    norms = squares(points)
    block_rows = min(1024, NPTS)

    def block_sums(index):
        offset = (index * block_rows).astype(jnp.int32)
        part_rows = lax.dynamic_slice_in_dim(points, offset, block_rows, 0)
        part_norms = lax.dynamic_slice_in_dim(norms, offset, block_rows, 0)
        inner_prod = lax.dot_general(part_rows, points, (((1,), (1,)), ((), ())), preferred_element_type=jnp.float32)
        squared = part_norms[:, None] + norms[None, :] - 2.0 * inner_prod
        tile_vals = jnp.exp(-squared / D).astype(jnp.bfloat16)
        return jnp.dot(tile_vals, indicator, preferred_element_type=jnp.float32)

    row_sums = lax.map(block_sums, jnp.arange(NPTS // block_rows, dtype=jnp.int32)).reshape(NPTS, CL)
    weights = indicator.astype(jnp.float32)
    counts = jnp.sum(weights, axis=0)
    self_total = jnp.sum(weights * row_sums, axis=0)
    sizes_floor = jnp.maximum(counts, 1.0)
    return 1.0 - 2.0 * row_sums / sizes_floor[None, :] + self_total[None, :] / (sizes_floor * sizes_floor)[None, :]
```

```python
import jax
import jax.numpy as jnp
from jax import lax
from jax.experimental import pallas as pl
from jax.experimental.pallas import tpu as pltpu
from jax.sharding import PartitionSpec as P

D = 768
CL = 128
PD = 64
SLOT = 4
NX, NY, NZ, ZL = 4, 4, 16, 4
SETS = 8
ROWS = 2048
RT = 512
MESH = pl.DeviceIdType.MESH
F32 = jnp.float32
BF = jnp.bfloat16


def iota(shape, dim):
    return lax.broadcasted_iota(jnp.int32, shape, dim)


def nt_dot(left, right):
    return lax.dot_general(left, right, (((1,), (1,)), ((), ())), preferred_element_type=F32)


def kernel(p_ref, a_ref, o_ref, zb, zm, seld, selo, gb, yo, ids, rowb, ind, nrow, ncol, nleft,
           self_acc, cnt_acc, zr_sem, zmr_sem, yd_sem, yo_sem, x_sem, xl_sem, id_sem,
           rr_sem, rp_sem, send_sem, rsend_sem):
    r = lax.axis_index("row")
    c = lax.axis_index("col")
    x = lax.rem(r, NX)
    zh = r // NX
    y = c // (2 * ZL)
    zl = lax.rem(c // 2, ZL)
    k = lax.rem(c, 2)
    z = zh * ZL + zl

    def dev(dx, dy, dz, other):
        nx = lax.rem(x + dx, NX)
        ny = lax.rem(y + dy, NY)
        nz = lax.rem(z + dz, NZ)
        nk = 1 - k if other is True else (k if other is False else other)
        return (nz // ZL * NX + nx, (ny * ZL + lax.rem(nz, ZL)) * 2 + nk)

    right, left = dev(0, 0, 1, False), dev(0, 0, NZ - 1, False)
    partner = dev(0, 0, 0, True)
    pending = []
    count = [0]

    def send(src, dst, recv, device):
        sem = send_sem.at[count[0]]
        count[0] += 1
        cp = pltpu.make_async_remote_copy(src, dst, sem, recv, device_id=device, device_id_type=MESH)
        cp.start()
        pending.append(cp)

    def arrived(dst, recv):
        pltpu.make_async_copy(dst, dst, recv).wait()

    yo[...] = jnp.zeros_like(yo)
    barrier = pltpu.get_barrier_semaphore()
    peers = [right, left, partner]
    for dy in (1, 2, 3):
        peers += [dev(0, dy, 0, False), dev(0, dy, 0, True)]
    peers += [dev(dx, 0, 0, False) for dx in (1, 2, 3)]
    for peer in peers:
        pl.semaphore_signal(barrier, inc=1, device_id=peer, device_id_type=MESH)

    arow = a_ref[...]
    diag = iota((PD, PD), 0) == iota((PD, PD), 1)

    def to_col(row):
        return jnp.sum(jnp.where(diag, jnp.broadcast_to(row, (PD, PD)), 0), axis=1, keepdims=True)

    grow = arow // CL
    lrow = arow - grow * CL
    gcol = to_col(grow)
    earlier = (gcol == grow) & (iota((PD, PD), 0) < iota((PD, PD), 1))
    pos = jnp.sum(earlier.astype(jnp.int32), axis=0, keepdims=True)
    target = (grow * SLOT + pos).astype(F32)
    both = jnp.concatenate([target, lrow.astype(F32)], axis=1)
    zm[0, 0] = jnp.broadcast_to(both, (8, 2 * PD)).astype(BF)
    pl.semaphore_wait(barrier, len(peers))

    H = PD // 2

    def blk(s, b):
        return p_ref if (s, b) == (0, 0) else zb.at[s, b]

    def ring(s, b, half, ns, nb, device):
        send(blk(s, b).at[pl.ds(half * H, H)], zb.at[ns, nb, pl.ds(half * H, H)],
             zr_sem.at[ns, nb, half], device)

    def ring_meta(s, b, ns, nb, device):
        send(zm.at[s, b], zm.at[ns, nb], zmr_sem.at[ns, nb], device)

    def row_sends(s, b, m):
        src = blk(s, b)
        at = pl.multiple_of(((y * ZL + m) * 2 + k) * PD, PD)
        dst = rowb.at[pl.ds(at, PD)]
        pltpu.make_async_copy(src, dst, rr_sem.at[0, m]).start()
        pltpu.make_async_remote_copy(src, dst, rsend_sem.at[0, m], rp_sem.at[0, m],
                                     device_id=partner, device_id_type=MESH).start()
        for dy in (1, 2, 3):
            pltpu.make_async_remote_copy(src, dst, rsend_sem.at[dy, m], rr_sem.at[dy, m],
                                         device_id=dev(0, dy, 0, False), device_id_type=MESH).start()

    def row_at(dy, m, core):
        ys = lax.rem(y + NY - dy, NY)
        return rowb.at[pl.ds(pl.multiple_of(((ys * ZL + m) * 2 + core) * PD, PD), PD)]

    for half in (0, 1):
        ring(0, 0, half, 1, 0, right)
        ring(0, 0, half, 0, 1, left)
        if half == 0:
            ring_meta(0, 0, 1, 0, right)
            ring_meta(0, 0, 0, 1, left)

    def ring_step(s):
        for half in (0, 1):
            arrived(zb.at[s, 1, pl.ds(half * H, H)], zr_sem.at[s, 1, half])
            if s < SETS - 1:
                ring(s, 1, half, s + 1, 1, left)
            if s > 0:
                arrived(zb.at[s, 0, pl.ds(half * H, H)], zr_sem.at[s, 0, half])
                if s < SETS - 1:
                    ring(s, 0, half, s + 1, 0, right)
            if half == 0:
                arrived(zm.at[s, 1], zmr_sem.at[s, 1])
                if s < SETS - 1:
                    ring_meta(s, 1, s + 1, 1, left)
                if s > 0:
                    arrived(zm.at[s, 0], zmr_sem.at[s, 0])
                    if s < SETS - 1:
                        ring_meta(s, 0, s + 1, 0, right)

    def select(s):
        q = iota((PD, PD), 0)
        dy, core, b, p = q // 16, q // 8 % 2, q // 4 % 2, q % 4
        want = ((lax.rem(y + dy, NY) * ZL + zl) * 2 + core) * SLOT + p
        data = jnp.zeros((PD, D), F32)
        hot = jnp.zeros((PD, CL), F32)
        for bb in (0, 1):
            meta = zm[s, bb][0:1].astype(F32).astype(jnp.int32)
            trow, lrow_ = meta[:, :PD], meta[:, PD:]
            pick = ((trow == want) & (b == bb)).astype(BF)
            local = (to_col(lrow_) == iota((PD, CL), 1)).astype(BF)
            data += jnp.dot(pick, blk(s, bb)[...], preferred_element_type=F32)
            hot += jnp.dot(pick, local, preferred_element_type=F32)
        seld[s] = data.astype(BF)
        selo[s] = hot.astype(BF)

    def dispatch(s):
        for dy in (1, 3, 2, 0):
            src = ((NY - dy) % NY * 2 + k) * 8
            for core in (0, 1):
                if dy == 0 and core == 1:
                    continue
                at = dy * 16 + core * 8
                if dy == 0:
                    dest = partner
                    off = pl.multiple_of((1 - k) * 8, 8)
                else:
                    dest = dev(0, dy, 0, core)
                    off = at
                to = pl.ds(pl.multiple_of(src, 8), 8)
                send(seld.at[s, pl.ds(off, 8)], gb.at[s, 0, to], yd_sem.at[s], dest)
                send(selo.at[s, pl.ds(off, 8)], yo.at[s, to], yo_sem.at[s], dest)
        off = pl.ds(pl.multiple_of(k * 8, 8), 8)
        pltpu.make_async_copy(seld.at[s, off], gb.at[s, 0, off], yd_sem.at[s]).start()
        pltpu.make_async_copy(selo.at[s, off], yo.at[s, off], yo_sem.at[s]).start()

    def x_step(s):
        arrived(gb.at[s, 0], yd_sem.at[s])
        arrived(yo.at[s, pl.ds(0, PD)], yo_sem.at[s])
        send(gb.at[s, 0], gb.at[s, 3], x_sem.at[s, 0], dev(1, 0, 0, False))
        send(gb.at[s, 0], gb.at[s, 1], x_sem.at[s, 1], dev(3, 0, 0, False))
        number = (iota((8, CL), 1) + 1).astype(F32).astype(BF)
        ids[s, 0] = nt_dot(number, yo[s])
        for dx in (1, 2, 3):
            send(ids.at[s, 0], ids.at[s, NX - dx], id_sem.at[s, dx - 1], dev(dx, 0, 0, False))

    def relay(s):
        arrived(gb.at[s, 3], x_sem.at[s, 0])
        lo, hi = pl.ds(0, H), pl.ds(H, H)
        send(gb.at[s, 3, lo], gb.at[s, 2, lo], xl_sem.at[s, 0], dev(1, 0, 0, False))
        arrived(gb.at[s, 1], x_sem.at[s, 1])
        send(gb.at[s, 1, hi], gb.at[s, 2, hi], xl_sem.at[s, 1], dev(3, 0, 0, False))

    def x_done(s):
        arrived(gb.at[s, 2, pl.ds(0, H)], xl_sem.at[s, 0])
        arrived(gb.at[s, 2, pl.ds(H, H)], xl_sem.at[s, 1])
        for dx in (1, 2, 3):
            arrived(ids.at[s, NX - dx], id_sem.at[s, dx - 1])

    def row_relay():
        for dy in (1, 3, 2):
            for m in range(ZL):
                ref = row_at(dy, m, k)
                arrived(ref, rr_sem.at[dy, m])
                send(ref, ref, rp_sem.at[dy, m], partner)

    def row_done():
        for m in range(ZL):
            arrived(row_at(0, m, k), rr_sem.at[0, m])
            for dy in range(NY):
                arrived(row_at(dy, m, 1 - k), rp_sem.at[dy, m])

    inv = 1.0 / D

    def prepare(s):
        def wide(a, b):
            return a + pltpu.roll(b, PD, 1)
        row = jnp.concatenate([wide(ids[s, 0], ids[s, 1]), wide(ids[s, 2], ids[s, 3])], axis=1)
        hot = (row[0:1].astype(jnp.int32) - 1 == iota((CL, 256), 0)).astype(F32)
        ind[s] = hot.T.astype(BF)
        cnt_acc[...] += jnp.broadcast_to(jnp.sum(ind[s].astype(F32), axis=0, keepdims=True), (8, CL))
        g = gb[s].reshape(256, D).astype(F32)
        sq = g * g
        hi = sq.astype(BF)
        lo = (sq - hi.astype(F32)).astype(BF)
        ones = jnp.ones((8, D), BF)
        nrow[s] = (nt_dot(ones, hi) + nt_dot(ones, lo)) * inv
        ncol[s] = jnp.broadcast_to(jnp.sum(sq, axis=1, keepdims=True) * inv, (256, CL))

    def tile(lrows, lnorm, s):
        g = gb[s].reshape(256, D)
        prod = nt_dot(lrows, g)
        norm = jnp.concatenate([lnorm, lnorm], axis=1)
        kern = jnp.exp(prod * (2.0 * inv) - (norm + nrow[s][0:1])).astype(BF)
        return jnp.dot(kern, ind[s], preferred_element_type=F32)

    def self_sums(s, t):
        sums = tile(gb[t].reshape(256, D), ncol[t], s)
        return jnp.sum(ind[t].astype(F32) * sums, axis=0, keepdims=True)

    for s in range(SETS + 3):
        if s < SETS:
            ring_step(s)
            select(s)
            dispatch(s)
            for b, m in ((0, zl - s), (1, zl + s + 1)):
                if s < ZL:
                    pl.when((m >= 0) & (m < ZL))(lambda b=b, m=m, s=s: row_sends(s, b, m))
        if 1 <= s <= SETS:
            x_step(s - 1)
        if 2 <= s <= SETS + 1:
            relay(s - 2)
        if s == 6:
            row_relay()
        if 3 <= s:
            x_done(s - 3)
    row_done()

    for t in range(ROWS // RT):
        rows = pl.ds(t * RT, RT)
        v = rowb[rows, :].astype(F32)
        nleft[rows, :] = jnp.broadcast_to(jnp.sum(v * v, axis=1, keepdims=True) * inv, (RT, CL))
    o_ref[...] = jnp.zeros_like(o_ref)
    self_acc[...] = jnp.zeros_like(self_acc)
    cnt_acc[...] = jnp.zeros_like(cnt_acc)

    def per_set(s, carry):
        prepare(s)

        def per_rows(t, carry):
            rows = pl.ds(pl.multiple_of(t * RT, RT), RT)
            o_ref[rows, :] += tile(rowb[rows, :], nleft[rows, :], s)
            return carry

        lax.fori_loop(0, ROWS // RT, per_rows, 0)
        total = lax.fori_loop(0, s, lambda t, acc: acc + 2.0 * self_sums(s, t), self_sums(s, s))
        self_acc[...] += jnp.broadcast_to(total, (8, CL))
        return carry

    lax.fori_loop(0, SETS, per_set, 0)

    m_inv = 1.0 / jnp.maximum(cnt_acc[0:1], 1.0)
    base = 1.0 + self_acc[0:1] * (m_inv * m_inv)
    slope = 2.0 * m_inv

    def finish(t, carry):
        rows = pl.ds(pl.multiple_of(t * RT, RT), RT)
        o_ref[rows, :] = base - slope * o_ref[rows, :]
        return carry

    lax.fori_loop(0, ROWS // RT, finish, 0)

    for cp in pending:
        cp.wait_send()
    for m in range(ZL):
        for dy in range(NY):
            dst = row_at(0, m, k)
            pltpu.make_async_remote_copy(dst, dst, rsend_sem.at[dy, m], rr_sem.at[dy, m],
                                         device_id=partner, device_id_type=MESH).wait_send()


def per_device(points, assign):
    dma = pltpu.SemaphoreType.DMA
    vmem = pltpu.VMEM
    return pl.pallas_call(
        kernel,
        out_shape=jax.ShapeDtypeStruct((ROWS, CL), F32),
        in_specs=[pl.BlockSpec(memory_space=pltpu.VMEM)] * 2,
        out_specs=pl.BlockSpec(memory_space=pltpu.VMEM),
        scratch_shapes=[
            vmem((SETS, 2, PD, D), BF),
            vmem((SETS, 2, 8, 2 * PD), BF),
            vmem((SETS, PD, D), BF),
            vmem((SETS, PD, CL), BF),
            vmem((SETS, NX, PD, D), BF),
            vmem((SETS, CL, CL), BF),
            vmem((SETS, NX, 8, CL), F32),
            vmem((ROWS, D), BF),
            vmem((SETS, 256, CL), BF),
            vmem((SETS, 8, 256), F32),
            vmem((SETS, 256, CL), F32),
            vmem((ROWS, CL), F32),
            vmem((8, CL), F32),
            vmem((8, CL), F32),
            dma((SETS, 2, 2)),
            dma((SETS, 2)),
            dma((SETS,)),
            dma((SETS,)),
            dma((SETS, 2)),
            dma((SETS, 2)),
            dma((SETS, 3)),
            dma((NY, ZL)),
            dma((NY, ZL)),
            dma((320,)),
            dma((NY, ZL)),
        ],
        compiler_params=pltpu.CompilerParams(
            collective_id=0, has_side_effects=True, vmem_limit_bytes=60 * 1024 * 1024
        ),
        name="kmeans",
    )(points, assign.reshape(1, PD))


def solution(mesh):
    return jax.shard_map(
        per_device,
        mesh=mesh,
        in_specs=(P(("row", "col"), None), P(("row", "col"))),
        out_specs=P("row", "col"),
        check_vma=False,
    )
```

```python
import jax
import jax.numpy as jnp
from jax import lax
from jax.experimental import pallas as pl
from jax.experimental.pallas import tpu as pltpu
from jax.sharding import PartitionSpec as P

D = 768
CL = 128
PD = 64
SLOT = 4
NX, NY, NZ, ZL = 4, 4, 16, 4
SETS = 8
ROWS = 2048
CHUNKS = 4
PAIR = 512
MESH = pl.DeviceIdType.MESH
F32 = jnp.float32
BF = jnp.bfloat16


def iota(shape, dim):
    return lax.broadcasted_iota(jnp.int32, shape, dim)


def nt_dot(left, right):
    return lax.dot_general(left, right, (((1,), (1,)), ((), ())), preferred_element_type=F32)


def kernel(p_ref, a_ref, o_ref, zb, zm, seld, selo, gb, yo, ids, rowb, ind, nrow, nown, nleft,
           self_acc, cnt_acc, part, zr_sem, zmr_sem, yd_sem, yo_sem, x_sem, xl_sem, id_sem,
           rr_sem, rp_sem, part_sem, send_sem, rsend_sem, psend_sem):
    r = lax.axis_index("row")
    c = lax.axis_index("col")
    x = lax.rem(r, NX)
    zh = r // NX
    y = c // (2 * ZL)
    zl = lax.rem(c // 2, ZL)
    k = lax.rem(c, 2)
    z = zh * ZL + zl

    def dev(dx, dy, dz, other):
        nx = lax.rem(x + dx, NX)
        ny = lax.rem(y + dy, NY)
        nz = lax.rem(z + dz, NZ)
        nk = 1 - k if other is True else (k if other is False else other)
        return (nz // ZL * NX + nx, (ny * ZL + lax.rem(nz, ZL)) * 2 + nk)

    inv = 1.0 / D
    right, left = dev(0, 0, 1, False), dev(0, 0, NZ - 1, False)
    partner = dev(0, 0, 0, True)
    pending = []
    count = [0]

    def send(src, dst, recv, device):
        sem = send_sem.at[count[0]]
        count[0] += 1
        cp = pltpu.make_async_remote_copy(src, dst, sem, recv, device_id=device, device_id_type=MESH)
        cp.start()
        pending.append(cp)

    def arrived(dst, recv):
        pltpu.make_async_copy(dst, dst, recv).wait()

    yo[...] = jnp.zeros_like(yo)
    self_acc[...] = jnp.zeros_like(self_acc)
    cnt_acc[...] = jnp.zeros_like(cnt_acc)
    barrier = pltpu.get_barrier_semaphore()
    peers = [right, left, partner]
    for dy in (1, 2, 3):
        peers += [dev(0, dy, 0, False), dev(0, dy, 0, True)]
    peers += [dev(dx, 0, 0, False) for dx in (1, 2, 3)]
    for peer in peers:
        pl.semaphore_signal(barrier, inc=1, device_id=peer, device_id_type=MESH)

    arow = a_ref[...]
    diag = iota((PD, PD), 0) == iota((PD, PD), 1)

    def to_col(row):
        return jnp.sum(jnp.where(diag, jnp.broadcast_to(row, (PD, PD)), 0), axis=1, keepdims=True)

    grow = arow // CL
    lrow = arow - grow * CL
    gcol = to_col(grow)
    earlier = (gcol == grow) & (iota((PD, PD), 0) < iota((PD, PD), 1))
    pos = jnp.sum(earlier.astype(jnp.int32), axis=0, keepdims=True)
    target = (grow * SLOT + pos).astype(F32)
    both = jnp.concatenate([target, lrow.astype(F32)], axis=1)
    zm[0, 0] = jnp.broadcast_to(both, (8, 2 * PD)).astype(BF)
    pl.semaphore_wait(barrier, len(peers))

    H = PD // 2
    Q = PD // CHUNKS

    def blk(s, b):
        return p_ref if (s, b) == (0, 0) else zb.at[s, b]

    def ring(s, b, half, ns, nb, device):
        send(blk(s, b).at[pl.ds(half * Q, Q)], zb.at[ns, nb, pl.ds(half * Q, Q)],
             zr_sem.at[ns, nb, half], device)

    def ring_meta(s, b, ns, nb, device):
        send(zm.at[s, b], zm.at[ns, nb], zmr_sem.at[ns, nb], device)

    nearest = ((0, 1, 2, 3), (0, 1, -1, 2), (0, 1, -1, -2), (0, -1, -2, -3))

    def by_zl(fn):
        for v in range(ZL):
            pl.when(zl == v)(lambda v=v: fn(v))

    def row_sends(i, dys):
        def go(v):
            d = nearest[v][i]
            m = v + d
            src = blk(-d, 0) if d <= 0 else blk(d - 1, 1)
            dst = row_at(0, m, k)
            for dy in dys:
                if dy == 0:
                    pltpu.make_async_copy(src, dst, rr_sem.at[0, m]).start()
                    pltpu.make_async_remote_copy(src, dst, rsend_sem.at[0, m], rp_sem.at[0, m],
                                                 device_id=partner, device_id_type=MESH).start()
                else:
                    pltpu.make_async_remote_copy(src, dst, rsend_sem.at[dy, m], rr_sem.at[dy, m],
                                                 device_id=dev(0, dy, 0, False),
                                                 device_id_type=MESH).start()
        by_zl(go)

    def row_pass(i, dys):
        def go(v):
            m = v + nearest[v][i]
            for dy in dys:
                ref = row_at(dy, m, k)
                arrived(ref, rr_sem.at[dy, m])
                pltpu.make_async_remote_copy(ref, ref, psend_sem.at[dy, m], rp_sem.at[dy, m],
                                             device_id=partner, device_id_type=MESH).start()
        by_zl(go)

    def row_at(dy, m, core):
        ys = lax.rem(y + NY - dy, NY)
        return rowb.at[pl.ds(pl.multiple_of(((ys * ZL + m) * 2 + core) * PD, PD), PD)]

    for half in range(CHUNKS):
        ring(0, 0, half, 1, 0, right)
        ring(0, 0, half, 0, 1, left)
        if half == 0:
            ring_meta(0, 0, 1, 0, right)
            ring_meta(0, 0, 0, 1, left)

    def ring_step(s):
        for half in range(CHUNKS):
            arrived(zb.at[s, 1, pl.ds(half * Q, Q)], zr_sem.at[s, 1, half])
            if s < SETS - 1:
                ring(s, 1, half, s + 1, 1, left)
            if s > 0:
                arrived(zb.at[s, 0, pl.ds(half * Q, Q)], zr_sem.at[s, 0, half])
                if s < SETS - 1:
                    ring(s, 0, half, s + 1, 0, right)
            if half == 0:
                arrived(zm.at[s, 1], zmr_sem.at[s, 1])
                if s < SETS - 1:
                    ring_meta(s, 1, s + 1, 1, left)
                if s > 0:
                    arrived(zm.at[s, 0], zmr_sem.at[s, 0])
                    if s < SETS - 1:
                        ring_meta(s, 0, s + 1, 0, right)

    def select(s):
        q = iota((PD, PD), 0)
        dy, core, b, p = q // 16, q // 8 % 2, q // 4 % 2, q % 4
        want = ((lax.rem(y + dy, NY) * ZL + zl) * 2 + core) * SLOT + p
        data = jnp.zeros((PD, D), F32)
        hot = jnp.zeros((PD, CL), F32)
        for bb in (0, 1):
            meta = zm[s, bb][0:1].astype(F32).astype(jnp.int32)
            trow, lrow_ = meta[:, :PD], meta[:, PD:]
            pick = ((trow == want) & (b == bb)).astype(BF)
            local = (to_col(lrow_) == iota((PD, CL), 1)).astype(BF)
            data += jnp.dot(pick, blk(s, bb)[...], preferred_element_type=F32)
            hot += jnp.dot(pick, local, preferred_element_type=F32)
        seld[s] = data.astype(BF)
        selo[s] = hot.astype(BF)

    def dispatch(s):
        for dy in (1, 3, 2, 0):
            src = ((NY - dy) % NY * 2 + k) * 8
            for core in (0, 1):
                if dy == 0 and core == 1:
                    continue
                at = dy * 16 + core * 8
                if dy == 0:
                    dest = partner
                    off = pl.multiple_of((1 - k) * 8, 8)
                else:
                    dest = dev(0, dy, 0, core)
                    off = at
                to = pl.ds(pl.multiple_of(src, 8), 8)
                send(seld.at[s, pl.ds(off, 8)], gb.at[s, 0, to], yd_sem.at[s], dest)
                send(selo.at[s, pl.ds(off, 8)], yo.at[s, to], yo_sem.at[s], dest)
        off = pl.ds(pl.multiple_of(k * 8, 8), 8)
        pltpu.make_async_copy(seld.at[s, off], gb.at[s, 0, off], yd_sem.at[s]).start()
        pltpu.make_async_copy(selo.at[s, off], yo.at[s, off], yo_sem.at[s]).start()

    def x_step(s):
        arrived(gb.at[s, 0], yd_sem.at[s])
        arrived(yo.at[s, pl.ds(0, PD)], yo_sem.at[s])
        send(gb.at[s, 0], gb.at[s, 3], x_sem.at[s, 0], dev(1, 0, 0, False))
        send(gb.at[s, 0], gb.at[s, 1], x_sem.at[s, 1], dev(3, 0, 0, False))
        number = (iota((8, CL), 1) + 1).astype(F32).astype(BF)
        v = gb[s, 0].astype(F32)
        sq = v * v
        hi = sq.astype(BF)
        lo = (sq - hi.astype(F32)).astype(BF)
        pad = jnp.zeros((PD, D), BF)
        ones = jnp.ones((8, D), BF)
        norm = nt_dot(ones, jnp.concatenate([hi, pad], axis=0)) + nt_dot(ones, jnp.concatenate([lo, pad], axis=0))
        ids[s, 0] = jnp.where(iota((8, CL), 0) == 0, nt_dot(number, yo[s]), norm * inv)
        nown[pl.ds(s * PD, PD), :] = jnp.broadcast_to(jnp.sum(sq, axis=1, keepdims=True) * inv, (PD, CL))
        for dx in (1, 2, 3):
            send(ids.at[s, 0], ids.at[s, NX - dx], id_sem.at[s, dx - 1], dev(dx, 0, 0, False))

    def relay(s):
        lo, hi = pl.ds(0, H), pl.ds(H, H)
        arrived(gb.at[s, 3], x_sem.at[s, 0])
        send(gb.at[s, 3, lo], gb.at[s, 2, lo], xl_sem.at[s, 0], dev(1, 0, 0, False))
        arrived(gb.at[s, 1], x_sem.at[s, 1])
        send(gb.at[s, 1, hi], gb.at[s, 2, hi], xl_sem.at[s, 1], dev(3, 0, 0, False))

    def x_done(s):
        arrived(gb.at[s, 2, pl.ds(0, H)], xl_sem.at[s, 0])
        arrived(gb.at[s, 2, pl.ds(H, H)], xl_sem.at[s, 1])
        for dx in (1, 2, 3):
            arrived(ids.at[s, NX - dx], id_sem.at[s, dx - 1])

    def tile_ready(dy):
        if dy == 0:
            for m in range(ZL):
                arrived(row_at(0, m, k), rr_sem.at[0, m])
        for m in range(ZL):
            arrived(row_at(dy, m, 1 - k), rp_sem.at[dy, m])
        rows = tile_rows(dy)
        v = rowb[rows, :].astype(F32)
        nleft[rows, :] = jnp.broadcast_to(jnp.sum(v * v, axis=1, keepdims=True) * inv, (PAIR, CL))

    def tile_rows(dy):
        return pl.ds(pl.multiple_of(lax.rem(y + NY - dy, NY) * PAIR, PAIR), PAIR)

    def prepare(s):
        def wide(row):
            ab = ids[s, 0, row:row + 1] + pltpu.roll(ids[s, 1, row:row + 1], PD, 1)
            cd = ids[s, 2, row:row + 1] + pltpu.roll(ids[s, 3, row:row + 1], PD, 1)
            return jnp.concatenate([ab, cd], axis=1)
        number = wide(0)
        hot = (number.astype(jnp.int32) - 1 == iota((CL, 256), 0)).astype(F32)
        ind[s] = hot.T.astype(BF)
        cnt_acc[...] += jnp.broadcast_to(jnp.sum(hot.T, axis=0, keepdims=True), (8, CL))
        nrow[s] = jnp.broadcast_to(wide(1), (8, 256))

    def tile(lrows, lnorm, s, n):
        g = gb[pl.ds(s, n)].reshape(n * 256, D)
        prod = nt_dot(lrows, g)
        right = jnp.concatenate([nrow[s + i][0:1] for i in range(n)], axis=1)
        norm = jnp.concatenate([lnorm] * (2 * n), axis=1)
        kern = jnp.exp(prod * (2.0 * inv) - (norm + right)).astype(BF)
        return jnp.dot(kern, ind[pl.ds(s, n)].reshape(n * 256, CL), preferred_element_type=F32)

    def unit(dy, s, n=2):
        rows = tile_rows(dy)
        o_ref[rows, :] += tile(rowb[rows, :], nleft[rows, :], s, n)

    def self_unit(s, n=2):
        own = gb[:, 0].reshape(PAIR, D)
        sums = tile(own, nown[...], s, n)
        hot = yo[:, 0:PD].reshape(PAIR, CL).astype(F32)
        self_acc[...] += jnp.broadcast_to(jnp.sum(hot * sums, axis=0, keepdims=True), (8, CL))

    o_ref[...] = jnp.zeros_like(o_ref)
    for s in range(SETS):
        ring_step(s)
        select(s)
        dispatch(s)
        if s < 4:
            row_sends(s, (0, 1, 3))
        if s >= 1:
            x_step(s - 1)
        if 3 <= s <= 6:
            row_sends(s - 3, (2,))
        if 2 <= s <= 5:
            row_pass(s - 2, (1, 3))
        if s == 4:
            tile_ready(0)
        if s == 6:
            tile_ready(1)
            tile_ready(3)
        if s >= 4:
            x_done(s - 4)
            prepare(s - 4)
        if s == 5:
            unit(0, 0)
        if s == 6:
            unit(1, 0)
        if s == 7:
            unit(3, 0)
        if s >= 2:
            relay(s - 2)

    relay(6)
    for i in range(4):
        row_pass(i, (2,))
    x_step(7)
    unit(0, 2)
    tile_ready(2)
    unit(2, 0)
    lax.fori_loop(1, 4, lambda i, carry: (unit(i, 2), carry)[1], 0)
    relay(7)
    for s in (4, 5):
        x_done(s)
        prepare(s)
    lax.fori_loop(0, 4, lambda i, carry: (unit(i, 4), carry)[1], 0)
    lax.fori_loop(0, 3, lambda i, carry: (self_unit(2 * i), carry)[1], 0)
    for s in (6, 7):
        x_done(s)
        prepare(s)
    self_unit(6)
    part[0] = self_acc[...]
    for dx in (1, 2, 3):
        send(part.at[0], part.at[NX - dx], part_sem.at[dx - 1], dev(dx, 0, 0, False))
    lax.fori_loop(0, 4, lambda i, carry: (unit(i, 6), carry)[1], 0)
    for dx in (1, 2, 3):
        arrived(part.at[NX - dx], part_sem.at[dx - 1])
    total = part[0] + part[1] + part[2] + part[3]

    m_inv = 1.0 / jnp.maximum(cnt_acc[0:1], 1.0)
    base = 1.0 + total[0:1] * (m_inv * m_inv)
    slope = 2.0 * m_inv

    def finish(t, carry):
        rows = pl.ds(pl.multiple_of(t * PAIR, PAIR), PAIR)
        o_ref[rows, :] = base - slope * o_ref[rows, :]
        return carry

    lax.fori_loop(0, ROWS // PAIR, finish, 0)

    for cp in pending:
        cp.wait_send()
    for m in range(ZL):
        dst = row_at(0, m, k)
        for dy in range(NY):
            sems = (rsend_sem,) if dy == 0 else (rsend_sem, psend_sem)
            for sem in sems:
                pltpu.make_async_remote_copy(dst, dst, sem.at[dy, m], rr_sem.at[dy, m],
                                             device_id=partner, device_id_type=MESH).wait_send()


def per_device(points, assign):
    dma = pltpu.SemaphoreType.DMA
    vmem = pltpu.VMEM
    return pl.pallas_call(
        kernel,
        out_shape=jax.ShapeDtypeStruct((ROWS, CL), F32),
        in_specs=[pl.BlockSpec(memory_space=pltpu.VMEM)] * 2,
        out_specs=pl.BlockSpec(memory_space=pltpu.VMEM),
        scratch_shapes=[
            vmem((SETS, 2, PD, D), BF),
            vmem((SETS, 2, 8, 2 * PD), BF),
            vmem((SETS, PD, D), BF),
            vmem((SETS, PD, CL), BF),
            vmem((SETS, NX, PD, D), BF),
            vmem((SETS, CL, CL), BF),
            vmem((SETS, NX, 8, CL), F32),
            vmem((ROWS, D), BF),
            vmem((SETS, 256, CL), BF),
            vmem((SETS, 8, 256), F32),
            vmem((SETS * PD, CL), F32),
            vmem((ROWS, CL), F32),
            vmem((8, CL), F32),
            vmem((8, CL), F32),
            vmem((NX, 8, CL), F32),
            dma((SETS, 2, CHUNKS)),
            dma((SETS, 2)),
            dma((SETS,)),
            dma((SETS,)),
            dma((SETS, 2)),
            dma((SETS, 2)),
            dma((SETS, 3)),
            dma((NY, ZL)),
            dma((NY, ZL)),
            dma((3,)),
            dma((400,)),
            dma((NY, ZL)),
            dma((NY, ZL)),
        ],
        compiler_params=pltpu.CompilerParams(
            collective_id=0, has_side_effects=True, vmem_limit_bytes=28 * 1024 * 1024
        ),
        name="kmeans",
    )(points, assign.reshape(1, PD))


def solution(mesh):
    return jax.shard_map(
        per_device,
        mesh=mesh,
        in_specs=(P(("row", "col"), None), P(("row", "col"))),
        out_specs=P("row", "col"),
        check_vma=False,
    )
```
